32 devices in a mesh: section: 2 (over core), ctx: 4 (over z), tensor: 4 (over y, x).
Axes of the slice: x: 2, y: 2, z: 4, core: 2. Of those that a mesh axis runs over, the one named last changes fastest.
Arguments:
- block_input: bfloat16 [2, 1024, 768], P(None, 'ctx'), may hold values from -6 to 6
- out_grad: bfloat16 [2, 1024, 768], P(None, 'ctx'), may hold values from -6 to 6
- norm_gain: bfloat16 [2, 768], P('section', 'ctx'), may hold values from 0.5 to 1.5
- w_zx: bfloat16 [2, 768, 2, 1536], P('section', 'ctx', None, 'tensor'), may hold values from -0.21875 to 0.21875
- w_bc: bfloat16 [2, 768, 256], P('section', 'ctx'), may hold values from -0.21875 to 0.21875
- w_dt: bfloat16 [2, 768, 24], P('section', 'ctx', 'tensor'), may hold values from -0.21875 to 0.21875
- conv_x: bfloat16 [2, 4, 24, 64], P('section', None, 'tensor', 'ctx'), may hold values from -3 to 3
- conv_x_bias: bfloat16 [2, 24, 64], P('section', 'tensor', 'ctx'), may hold values from -0.5 to 0.5
- conv_bc: bfloat16 [2, 4, 256], P('section', None, 'ctx'), may hold values from -3 to 3
- conv_bc_bias: bfloat16 [2, 256], P('section', 'ctx'), may hold values from -0.5 to 0.5
- head_params: float32 [2, 3, 24], P('section', None, 'tensor'), may hold values from -12 to 1.5, as said below
- gate_gain: bfloat16 [2, 24, 64], P('section', 'tensor', 'ctx'), may hold values from 0.5 to 1.5
- w_out: bfloat16 [2, 1536, 768], P('section', 'tensor', 'ctx'), may hold values from -0.15625 to 0.15625
Outputs:
- block_output: float32 [2, 2, 1024, 768], P('section', None, 'ctx')
- input_grad: float32 [2, 2, 1024, 768], P('section', None, 'ctx')
- norm_gain_grad: float32 [2, 768], P('section', 'ctx')
- w_zx_grad: float32 [2, 768, 2, 1536], P('section', 'ctx', None, 'tensor')
- w_bc_grad: float32 [2, 768, 256], P('section', 'ctx')
- w_dt_grad: float32 [2, 768, 24], P('section', 'ctx', 'tensor')
- conv_x_grad: float32 [2, 4, 24, 64], P('section', None, 'tensor', 'ctx')
- conv_x_bias_grad: float32 [2, 24, 64], P('section', 'tensor', 'ctx')
- conv_bc_grad: float32 [2, 4, 256], P('section', None, 'ctx')
- conv_bc_bias_grad: float32 [2, 256], P('section', 'ctx')
- head_params_grad: float32 [2, 3, 24], P('section', None, 'tensor')
- gate_gain_grad: float32 [2, 24, 64], P('section', 'tensor', 'ctx')
- w_out_grad: float32 [2, 1536, 768], P('section', 'tensor', 'ctx')
The draws below stay inside these ranges and needn't reach their ends.
Inputs may be any that keep to these rules, and one draw needn't show every extreme that they name: `head_params`: entry [s, 0, h] is added to head h's step sizes before softplus, entry [s, 1, h] is the logarithm of its decay rate, entry [s, 2, h] its skip weight.
All inputs are finite; a program needn't handle non-finite values.
Results may differ from the reference program's by a relative error of at most 0.019.
The reference program's roundings to bfloat16 on the way count: a program that leaves them out, or rounds other values in their place, can miss the bound.
Values may be sent and summed in bfloat16 or wider, within the bound.
No kernel may reach another device: no remote copies, remote signals or barrier semaphores. Data moves between devices by JAX's collectives and lax.ppermute only.
A program may use at most 128 MiB of HBM per device.

```python
import math
import jax
import jax.numpy as jnp
from jax import lax

D = 768
H = 24
P_SIZE = 64
N = 128
CONV = 4
BLOCK = 256
MICRO = 2
SEQ = 1024
DI = 1536


def draw_head_params(key, part):
    subkeys = jax.random.split(key, 5)
    fast_share = 0.5
    bias_low = -3.0
    bias_high = -2.0
    step_bias = jax.random.uniform(subkeys[0], (2, H), jnp.float32, bias_low, bias_high)
    is_fast = jax.random.uniform(subkeys[1], (2, H), jnp.float32) < fast_share
    slow_log = jax.random.uniform(subkeys[2], (2, H), jnp.float32, math.log(1.0 / SEQ), math.log(8.0 / SEQ))
    fast_log = jax.random.uniform(subkeys[3], (2, H), jnp.float32, math.log(0.15), math.log(0.3))
    rate_log = jnp.where(is_fast, fast_log, slow_log)
    skip_weight = jax.random.uniform(subkeys[4], (2, H), jnp.float32, 0.5, 1.5)
    return jnp.stack([step_bias, rate_log, skip_weight], axis=1)


def raised(entries, own_key, source, target, parts, factor):
    owner, partner = [(jnp.arange(entries.shape[axis_at]) // (entries.shape[axis_at] // parts)).reshape([-1 if axis == axis_at else 1 for axis in range(entries.ndim)]) for axis_at in (source, target)]
    chosen = jax.random.permutation(own_key, parts)[partner]
    strong = (owner == chosen) | (owner == (partner + parts // 2) % parts)
    return jnp.where(strong, factor * entries, entries)


def level_of(own_key, shape, cuts, smallest, high):
    level, own = 1.0, jax.random.fold_in(own_key, 6)
    for axis_at, shards_of in cuts:
        heights = jnp.exp(jax.random.uniform(jax.random.fold_in(own, axis_at), (shards_of,), jnp.float32, smallest / len(cuts), high / len(cuts)))
        level = level * jnp.repeat(heights, shape[axis_at] // shards_of).reshape([-1 if axis == axis_at else 1 for axis in range(len(shape))])
    return level


def noise(rng, extent, width, reach, cuts=(), kind=jnp.bfloat16):
    entries = width * jax.random.normal(rng, extent, jnp.float32)
    if cuts:
        entries = entries * level_of(rng, extent, cuts, -0.22, 0.18)
    return jnp.clip(entries, -reach, reach).astype(kind)


def bell_draw_with(own_key, extent, scale, limit, cuts, heavy, dtype=jnp.bfloat16):
    drawn = scale * jax.random.normal(own_key, extent, jnp.float32)
    if cuts:
        drawn = drawn * level_of(own_key, extent, cuts, -0.22, 0.18)
    return jnp.clip(raised(drawn, jax.random.fold_in(own_key, 3), *heavy), -limit, limit).astype(dtype)


def setup_inputs(seed: int = 0) -> dict:
    arg_keys = jax.random.split(jax.random.key(seed), 14)
    return {
        "block_input": noise(arg_keys[0], (MICRO, SEQ, D), 1.0, 6.0, ((1, 4),)),
        "out_grad": bell_draw_with(arg_keys[1], (MICRO, SEQ, D), 1.0, 6.0, ((1, 4),), (1, 2, 4, 2.0)),
        "norm_gain": jnp.clip(1.0 + 0.1 * jax.random.normal(arg_keys[2], (2, D), jnp.float32), 0.5, 1.5).astype(jnp.bfloat16),
        "w_zx": noise(arg_keys[3], (2, D, 2, DI), D ** -0.5, 0.21875, ((0, 2), (1, 4), (3, 4))),
        "w_bc": noise(arg_keys[4], (2, D, 2 * N), D ** -0.5, 0.21875, ((0, 2), (1, 4))),
        "w_dt": noise(arg_keys[5], (2, D, H), D ** -0.5, 0.21875, ((0, 2), (1, 4), (2, 4))),
        "conv_x": noise(arg_keys[6], (2, CONV, H, P_SIZE), CONV ** -0.5, 3.0, ((0, 2), (2, 4), (3, 4))),
        "conv_x_bias": jnp.clip(jax.random.uniform(arg_keys[7], (2, H, P_SIZE), jnp.float32, -0.5, 0.5) * level_of(arg_keys[7], (2, H, P_SIZE), ((0, 2), (1, 4), (2, 4)), -0.4, 0.0), -0.5, 0.5).astype(jnp.bfloat16),
        "conv_bc": noise(arg_keys[8], (2, CONV, 2 * N), CONV ** -0.5, 3.0, ((0, 2), (2, 4))),
        "conv_bc_bias": jnp.clip(jax.random.uniform(arg_keys[9], (2, 2 * N), jnp.float32, -0.5, 0.5) * level_of(arg_keys[9], (2, 2 * N), ((0, 2), (1, 4)), -0.4, 0.0), -0.5, 0.5).astype(jnp.bfloat16),
        "head_params": draw_head_params(jax.random.fold_in(arg_keys[13], 71), 0),
        "gate_gain": jnp.clip(1.0 + 0.1 * jax.random.normal(arg_keys[11], (2, H, P_SIZE), jnp.float32), 0.5, 1.5).astype(jnp.bfloat16),
        "w_out": noise(arg_keys[12], (2, DI, D), DI ** -0.5, 0.15625, ((0, 2), (1, 4), (2, 4))),
    }


EPSILON = 1e-05
HIGHEST = lax.Precision.HIGHEST

def ssd_scan(x_input, b_rows, c_rows, step_size, decay_rate, skip_weight):
    length, head_count, head_width = x_input.shape
    block_count = length // BLOCK
    causal = jnp.arange(BLOCK)[:, None] >= jnp.arange(BLOCK)[None, :]

    def advance(carried, pieces):
        x_block, b_block, c_block, step_block = pieces
        log_decay = jnp.cumsum(jnp.transpose(step_block * decay_rate), axis=1)
        scaled = x_block * step_block[:, :, None]
        spread = jnp.where(causal[None], log_decay[:, :, None] - log_decay[:, None, :], -1e+30)
        weights = jnp.exp(spread) * jnp.dot(c_block, jnp.transpose(b_block), precision=HIGHEST)[None]
        within = jnp.einsum('hij,jhp->ihp', weights, scaled, precision=HIGHEST)
        growth = jnp.transpose(jnp.exp(log_decay))
        across = jnp.einsum('in,hpn->ihp', c_block, carried, precision=HIGHEST) * growth[:, :, None]
        to_end = jnp.transpose(jnp.exp(log_decay[:, -1:] - log_decay))
        block_state = jnp.einsum('jhp,jn->hpn', scaled * to_end[:, :, None], b_block, precision=HIGHEST)
        carried = jnp.exp(log_decay[:, -1])[:, None, None] * carried + block_state
        return (carried, within + across + skip_weight[:, None] * x_block)
    initial = jnp.zeros((head_count, head_width, b_rows.shape[1]), jnp.float32)
    pieces = (x_input.reshape(block_count, BLOCK, head_count, head_width), b_rows.reshape(block_count, BLOCK, -1), c_rows.reshape(block_count, BLOCK, -1), step_size.reshape(block_count, BLOCK, head_count))
    final_state, outputs = lax.scan(advance, initial, pieces)
    return outputs.reshape(length, head_count, head_width)

def mixer_part(gate_raw, x_raw, bc_raw, dt_raw, conv_taps, conv_shift, head_table, gate_weight):
    length, channels = x_raw.shape
    kernel = conv_taps.shape[0]
    head_count = head_table.shape[1]
    state_size = bc_raw.shape[1] // 2
    conv_in = jnp.concatenate([x_raw, bc_raw], axis=1)
    extended = jnp.concatenate([jnp.zeros((kernel - 1, conv_in.shape[1]), jnp.float32), conv_in], axis=0)
    conv_pre = conv_shift + sum((conv_taps[offset] * extended[offset:offset + length] for offset in range(kernel)))
    conv_out = jax.nn.silu(conv_pre)
    x_input = conv_out[:, :channels].reshape(length, head_count, -1)
    b_rows = conv_out[:, channels:channels + state_size]
    c_rows = conv_out[:, channels + state_size:]
    step_size = jax.nn.softplus(dt_raw + head_table[0])
    decay_rate = -jnp.exp(head_table[1])
    ssd_out = ssd_scan(x_input, b_rows, c_rows, step_size, decay_rate, head_table[2]).reshape(length, channels)
    gated_out = ssd_out * jax.nn.silu(gate_raw)
    return gated_out * lax.rsqrt(lax.optimization_barrier(jnp.mean(gated_out * gated_out, axis=1, keepdims=True)) + EPSILON) * gate_weight

def norm_front(residual, gain):
    return residual * lax.rsqrt(lax.optimization_barrier(jnp.mean(residual * residual, axis=1, keepdims=True)) + EPSILON) * gain

def section_params(position, norm_gain, w_zx, w_bc, w_dt, conv_x, conv_x_bias, conv_bc, conv_bc_bias, head_params, gate_gain, w_out):
    kernel = conv_x.shape[1]
    conv_taps = jnp.concatenate([conv_x[position].reshape(kernel, -1), conv_bc[position]], axis=1).astype(jnp.float32)
    conv_shift = jnp.concatenate([conv_x_bias[position].reshape(-1), conv_bc_bias[position]]).astype(jnp.float32)
    return (norm_gain[position].astype(jnp.float32), w_zx[position], w_bc[position], w_dt[position], conv_taps, conv_shift, head_params[position], gate_gain[position].reshape(-1).astype(jnp.float32), w_out[position])

def block_pass(params, residual):
    norm_weight, proj_zx, proj_bc, proj_dt, conv_taps, conv_shift, head_table, gate_weight, proj_out = params
    length = residual.shape[0]
    model_width = proj_zx.shape[0]
    normed_f, front_back = jax.vjp(norm_front, residual, norm_weight)
    normed_in = normed_f.astype(jnp.bfloat16)
    flat_zx = proj_zx.reshape(model_width, -1)
    projected = jnp.dot(normed_in, flat_zx, preferred_element_type=jnp.float32).reshape(length, 2, -1)
    bc_raw = jnp.dot(normed_in, proj_bc, preferred_element_type=jnp.float32)
    dt_raw = jnp.dot(normed_in, proj_dt, preferred_element_type=jnp.float32)
    mixed_f, mixer_back = jax.vjp(mixer_part, projected[:, 0], projected[:, 1], bc_raw, dt_raw, conv_taps, conv_shift, head_table, gate_weight)
    mixed_out = mixed_f.astype(jnp.bfloat16)
    result = residual + jnp.dot(mixed_out, proj_out, preferred_element_type=jnp.float32)

    def backward(cotangent):
        grad_q = cotangent.astype(jnp.bfloat16)
        grad_out_w = jnp.dot(jnp.transpose(mixed_out), grad_q, preferred_element_type=jnp.float32)
        grad_mixed = jnp.dot(grad_q, jnp.transpose(proj_out), preferred_element_type=jnp.float32)
        grad_gate, grad_x, grad_bc, grad_dt, grad_taps, grad_shift, grad_heads, grad_gate_w = mixer_back(grad_mixed)
        grad_zx_b = jnp.stack([grad_gate, grad_x], axis=1).astype(jnp.bfloat16).reshape(length, -1)
        grad_bc_b = grad_bc.astype(jnp.bfloat16)
        grad_dt_b = grad_dt.astype(jnp.bfloat16)
        grad_zx_w = jnp.dot(jnp.transpose(normed_in), grad_zx_b, preferred_element_type=jnp.float32).reshape(proj_zx.shape)
        grad_bc_w = jnp.dot(jnp.transpose(normed_in), grad_bc_b, preferred_element_type=jnp.float32)
        grad_dt_w = jnp.dot(jnp.transpose(normed_in), grad_dt_b, preferred_element_type=jnp.float32)
        grad_normed = jnp.dot(grad_zx_b, jnp.transpose(flat_zx), preferred_element_type=jnp.float32) + jnp.dot(grad_bc_b, jnp.transpose(proj_bc), preferred_element_type=jnp.float32) + jnp.dot(grad_dt_b, jnp.transpose(proj_dt), preferred_element_type=jnp.float32)
        grad_resid, grad_norm = front_back(grad_normed)
        return (cotangent + grad_resid, (grad_norm, grad_zx_w, grad_bc_w, grad_dt_w, grad_taps, grad_shift, grad_heads, grad_gate_w, grad_out_w))
    return (result, backward)

def reference(block_input, out_grad, norm_gain, w_zx, w_bc, w_dt, conv_x, conv_x_bias, conv_bc, conv_bc_bias, head_params, gate_gain, w_out):
    micro_count = block_input.shape[0]
    sections = [section_params(position, norm_gain, w_zx, w_bc, w_dt, conv_x, conv_x_bias, conv_bc, conv_bc_bias, head_params, gate_gain, w_out) for position in range(2)]
    first_rows, second_rows, first_grads, second_grads = ([], [], [], [])
    totals = [None, None]
    for micro_index in range(micro_count):
        first_out, first_back = block_pass(sections[0], block_input[micro_index].astype(jnp.float32))
        second_out, second_back = block_pass(sections[1], first_out)
        second_grad, second_terms = second_back(out_grad[micro_index].astype(jnp.float32))
        first_grad, first_terms = first_back(second_grad)
        first_rows.append(first_out)
        second_rows.append(second_out)
        first_grads.append(first_grad)
        second_grads.append(second_grad)
        for position, terms in ((0, first_terms), (1, second_terms)):
            totals[position] = terms if totals[position] is None else jax.tree.map(jnp.add, totals[position], terms)
    kernel, head_count, head_width = (conv_x.shape[1], conv_x.shape[2], conv_x.shape[3])
    channels = head_count * head_width
    pieces = []
    for position in range(2):
        grad_norm, grad_zx_w, grad_bc_w, grad_dt_w, grad_taps, grad_shift, grad_heads, grad_gate_w, grad_out_w = totals[position]
        pieces.append((grad_norm, grad_zx_w, grad_bc_w, grad_dt_w, grad_taps[:, :channels].reshape(kernel, head_count, head_width), grad_shift[:channels].reshape(head_count, head_width), grad_taps[:, channels:], grad_shift[channels:], grad_heads, grad_gate_w.reshape(head_count, head_width), grad_out_w))
    stacked = [jnp.stack([pieces[0][slot], pieces[1][slot]]) for slot in range(11)]
    block_output = jnp.stack([jnp.stack(first_rows), jnp.stack(second_rows)])
    input_grad = jnp.stack([jnp.stack(first_grads), jnp.stack(second_grads)])
    return (block_output, input_grad, stacked[0], stacked[1], stacked[2], stacked[3], stacked[4], stacked[5], stacked[6], stacked[7], stacked[8], stacked[9], stacked[10])
```

```python
import functools

import jax
import jax.numpy as jnp
from jax import lax
from jax.experimental import pallas as pl
from jax.experimental.pallas import tpu as pltpu
from jax.sharding import PartitionSpec as P


EPSILON = 1e-05
F32 = jnp.float32
BF16 = jnp.bfloat16
LANES = 128
HALO = 16
SECTION, CTX, TENSOR = "section", "ctx", "tensor"
ROWS, GAIN, GATE, TABLE = 16, 5, 6, 8
VMEM_LIMIT = 28 * 1024 * 1024


def dot(a, b, contract):
    return lax.dot_general(
        a, b, ((contract[:1], contract[1:]), ((), ())), preferred_element_type=F32
    )


def mm(a, b):
    return dot(a.astype(BF16), b.astype(BF16), (1, 0))


def mm_nt(a, b):
    return dot(a.astype(BF16), b.astype(BF16), (1, 1))


def mm_tn(a, b):
    return dot(a.astype(BF16), b.astype(BF16), (0, 0))


def sigmoid(a):
    return 0.5 + 0.5 * jnp.tanh(0.5 * a)


def small_sigmoid(a):
    return 1.0 / (1.0 + jnp.exp(-a))


def softplus(a):
    return jnp.maximum(a, 0.0) + jnp.log1p(jnp.exp(-jnp.abs(a)))


def low_half(width):
    return lax.broadcasted_iota(jnp.int32, (1, LANES), 1) < width


def expand(columns, heads, width):
    low = low_half(width)
    tiles = [
        jnp.where(low, columns[:, h : h + 1], columns[:, h + 1 : h + 2]) for h in range(0, heads, 2)
    ]
    return jnp.concatenate(tiles, axis=1)


def head_sums(values, heads, width):
    channels = heads * width
    row = lax.broadcasted_iota(jnp.int32, (channels, LANES), 0) // width
    lane = lax.broadcasted_iota(jnp.int32, (channels, LANES), 1)
    select = (row == lane).astype(BF16)
    high = values.astype(BF16)
    low = (values - high.astype(F32)).astype(BF16)
    return dot(high, select, (1, 0)) + dot(low, select, (1, 0))


def ordered_sums(mask, values):
    high = values.astype(BF16)
    middle = (values - high.astype(F32)).astype(BF16)
    low = (values - high.astype(F32) - middle.astype(F32)).astype(BF16)
    ones = mask.astype(BF16)
    return dot(ones, high, (1, 0)) + (dot(ones, middle, (1, 0)) + dot(ones, low, (1, 0)))


def log_rows(last):
    high = last.astype(BF16).astype(F32)
    middle = (last - high).astype(BF16).astype(F32)
    low = last - high - middle
    row = lax.broadcasted_iota(jnp.int32, (HALO, LANES), 0)
    return jnp.where(row == 0, high, jnp.where(row == 1, middle, jnp.where(row == 2, low, 0.0)))


def combine(states, heads, width):
    channels = heads * width
    total = jnp.zeros((channels, LANES), F32)
    passed = jnp.zeros((1, LANES), F32)
    for state in states:
        weight = jnp.exp(passed)
        body = state[:channels, :].astype(F32)
        total = total + jnp.concatenate(
            [body[h * width : (h + 1) * width] * weight[:, h : h + 1] for h in range(heads)], axis=0
        )
        logs = state[channels:, :].astype(F32)
        passed = passed + logs[0:1] + logs[1:2] + logs[2:3]
    return total


def fetch(scalars, mine, others, target, sems):
    rows, columns = mine[0].shape
    count = len(mine)
    position, core = scalars[0], scalars[1]

    def copy(source, k, half, sem):
        owner = lax.rem(position - k + count, count)
        row = pl.multiple_of(owner * rows, HALO)
        column = pl.multiple_of(half * columns, LANES)
        return pltpu.make_async_copy(source, target.at[pl.ds(row, rows), pl.ds(column, columns)], sem)

    copies = [copy(mine[k], k, core, sems.at[0, k]) for k in range(count)]
    copies += [copy(others[k], k, 1 - core, sems.at[1, k]) for k in range(count)]
    for each in copies:
        each.start()
    return copies


def project_kernel(section, heads, width, kernel, count, scalars, u, halo, table, *refs):
    blocks, mine, others = refs[:count], refs[count : 2 * count], refs[2 * count : 3 * count]
    weights, params, normed, conv_in, conv_pre, dt_raw, logs, state, sems = refs[3 * count :]
    waits = fetch(scalars, mine, others, weights, sems)
    length = u.shape[0]
    channels = heads * width
    mixed_width = conv_in.shape[1]
    params[...] = sum(ref[section * ROWS : (section + 1) * ROWS, :].astype(F32) for ref in blocks)
    gain = params[GAIN : GAIN + 1, :]
    for ref, at in ((halo, 0), (u, HALO)):
        rows = ref[...].astype(F32)
        inv = lax.rsqrt(jnp.mean(rows * rows, axis=1, keepdims=True) + EPSILON)
        normed[at : at + rows.shape[0], :] = (rows * inv * gain).astype(BF16)
    for wait in waits:
        wait.wait()
    rest = dot(normed[...], weights[...], (1, 0))
    conv_in[...] = rest[:, :mixed_width]
    dt = rest[HALO:, mixed_width:]
    dt_raw[...] = dt
    pre = jnp.broadcast_to(params[kernel : kernel + 1, :mixed_width], (length, mixed_width))
    for k in range(kernel):
        pre = pre + params[k : k + 1, :mixed_width] * conv_in[pl.ds(HALO - kernel + 1 + k, length), :]
    conv_pre[...] = pre
    out = pre * sigmoid(pre)
    step = softplus(dt + table[0:1, :])
    rate = -jnp.exp(table[1:2, :])
    row = lax.broadcasted_iota(jnp.int32, (length, length), 0)
    column = lax.broadcasted_iota(jnp.int32, (length, length), 1)
    log_decay = ordered_sums(row >= column, step * rate)
    logs[...] = log_decay
    last = log_decay[length - 1 :, :]
    scaled = out[:, :channels] * expand(step * jnp.exp(last - log_decay), heads, width)
    state_size = (mixed_width - channels) // 2
    state[:channels, :] = mm_tn(scaled, out[:, channels : channels + state_size]).astype(BF16)
    state[channels:, :] = log_rows(last).astype(BF16)


def head_column(columns, h):
    lane = lax.broadcasted_iota(jnp.int32, (1, LANES), 1)
    return jnp.sum(jnp.where(lane == h, columns, 0.0), axis=1, keepdims=True)


def pair_lanes(pair, width):
    return pl.ds(pl.multiple_of(pair * 2 * width, LANES), 2 * width)


def causal_mask(length):
    row = lax.broadcasted_iota(jnp.int32, (length, length), 0)
    column = lax.broadcasted_iota(jnp.int32, (length, length), 1)
    return row >= column


def within_kernel(heads, width, count, scalars, conv_pre, dt_raw, logs, table, normed, *refs):
    mine, others = refs[:count], refs[count : 2 * count]
    within, weights, gate, sems, scaled, flipped = refs[2 * count :]
    waits = fetch(scalars, mine, others, weights, sems)
    channels = heads * width
    state_size = (conv_pre.shape[1] - channels) // 2
    pre = conv_pre[...]
    out = pre * sigmoid(pre)
    b_rows = out[:, channels : channels + state_size]
    c_rows = out[:, channels + state_size :]
    step = softplus(dt_raw[...] + table[0:1, :])
    scaled[...] = (out[:, :channels] * expand(step, heads, width)).astype(BF16)
    products = mm_nt(c_rows, b_rows)
    log_decay = logs[...]
    flipped[...] = jnp.transpose(log_decay)
    causal = causal_mask(pre.shape[0])
    low = low_half(width)

    @pl.loop(0, heads // 2)
    def _(pair):
        lanes = pair_lanes(pair, width)
        tile = scaled[:, lanes]
        parts = []
        for i in range(2):
            h = 2 * pair + i
            spread = head_column(log_decay, h) - flipped[pl.ds(h, 1), :]
            parts.append(mm(jnp.exp(jnp.where(causal, spread, -1e30)) * products, tile))
        within[:, lanes] = jnp.where(low, parts[0], parts[1])

    for wait in waits:
        wait.wait()
    gate[...] = dot(normed[HALO:, :], weights[:, :channels], (1, 0))


def squares_rows(total, length):
    row = lax.broadcasted_iota(jnp.int32, (HALO, length), 0)
    high = total.astype(BF16).astype(F32)
    middle = (total - high).astype(BF16).astype(F32)
    low = total - high - middle
    return jnp.where(row == 0, high, jnp.where(row == 1, middle, jnp.where(row == 2, low, 0.0)))


def squares_of(block):
    rows = block.astype(F32)
    return rows[0:1] + rows[1:2] + rows[2:3]


def out_kernel(heads, width, within, conv_pre, gate, logs, table, params, weights, *refs):
    states = refs[:-5]
    incoming, ssd, part_a, part_b, part_h = refs[-5:]
    channels = heads * width
    length = within.shape[0]
    state_size = (conv_pre.shape[1] - channels) // 2
    start = combine([ref[...] for ref in states], heads, width)
    incoming[...] = start
    x_in, c_rows = conv_pre[:, :channels], conv_pre[:, channels + state_size :]
    x_in, c_rows = x_in * sigmoid(x_in), c_rows * sigmoid(c_rows)
    across = mm_nt(c_rows, start) * expand(jnp.exp(logs[...]), heads, width)
    value = within[...] + across + expand(table[2:3, :], heads, width) * x_in
    ssd[...] = value
    raw = gate[...]
    gated = value * (raw * sigmoid(raw))
    total = jnp.sum(gated * gated, axis=1, keepdims=True)
    total = jnp.transpose(jnp.broadcast_to(total, (length, LANES)))[0:1, :]
    part = mm_nt(gated * params[GATE : GATE + 1, :channels], weights[:, channels:])
    half = length // 2
    part_a[:half, :] = part[:half].astype(BF16)
    part_a[half:, :] = jnp.zeros((HALO, part_a.shape[1]), BF16)
    split = squares_rows(total, length).astype(BF16)
    part_a[half:, :length] = split
    part_b[...] = part[half:].astype(BF16)
    part_h[:HALO, :] = part[length - HALO :].astype(BF16)
    part_h[HALO:, :] = jnp.zeros((HALO, part_h.shape[1]), BF16)
    part_h[HALO:, :length] = split


def add_squares(first, second, length):
    total = squares_of(first[:, :length]) + squares_of(second[:, :length])
    return squares_rows(total, length).astype(BF16)


def first_sum_kernel(length, half, a0, a1, b0, b1, *refs):
    *tails, a, b = refs
    a[:half, :] = (a0[:half, :].astype(F32) + a1[:half, :].astype(F32)).astype(BF16)
    a[half:, :] = jnp.zeros((HALO, a.shape[1]), BF16)
    a[half:, :length] = add_squares(a0[half:, :], a1[half:, :], length)
    b[:half, :] = (b0[...].astype(F32) + b1[...].astype(F32)).astype(BF16)
    if tails:
        h0, h1 = tails
        b[half : half + HALO, :] = (h0[:HALO, :].astype(F32) + h1[:HALO, :].astype(F32)).astype(BF16)
        b[half + HALO :, :] = jnp.zeros((HALO, b.shape[1]), BF16)
        b[half + HALO :, :length] = add_squares(h0[HALO:, :], h1[HALO:, :], length)


def split_lanes(values):
    high = values.astype(BF16)
    middle = (values - high.astype(F32)).astype(BF16)
    low = (values - high.astype(F32) - middle.astype(F32)).astype(BF16)
    return jnp.concatenate([high, middle, low], axis=1)


def join_lanes(values, lanes):
    wide = values.astype(F32)
    return wide[:, :lanes] + wide[:, lanes : 2 * lanes] + wide[:, 2 * lanes : 3 * lanes]


def first_sum_back_kernel(both, half, a0, a1, b0, b1, h0, h1, a, b):
    a[:half, :] = (a0[:half, :].astype(F32) + a1[:half, :].astype(F32)).astype(BF16)
    a[half:, :] = jnp.zeros((HALO, a.shape[1]), BF16)
    a[half:, : 3 * both] = split_lanes(join_lanes(a0[half:, :], both) + join_lanes(a1[half:, :], both))
    added = b0[...].astype(F32) + b1[...].astype(F32)
    tail = h0[...].astype(F32) + h1[...].astype(F32)
    b[: half - HALO, :] = added[: half - HALO].astype(BF16)
    b[half - HALO :, :] = (added[half - HALO :] + tail).astype(BF16)


def column_of(total, length):
    return jnp.transpose(jnp.broadcast_to(total, (LANES, length)))[:, 0:1]


def add_kernel(width_total, half, u, a0, a1, b0, b1, *refs):
    length = u.shape[0]
    if len(refs) > 3:
        halo, result, sums, scale, next_halo = refs
        squares = squares_of(b0[half + HALO :, :length]) + squares_of(b1[half + HALO :, :length])
        factor = lax.rsqrt(column_of(squares, length) / width_total + EPSILON)[length - HALO :]
        rows = slice(half, half + HALO)
        added = b0[rows, :].astype(F32) + b1[rows, :].astype(F32)
        next_halo[...] = halo[...].astype(F32) + factor * added
    else:
        result, sums, scale = refs
    total = squares_of(a0[half:, :length]) + squares_of(a1[half:, :length])
    factor = lax.rsqrt(column_of(total, length) / width_total + EPSILON)
    scale[...] = jnp.broadcast_to(factor, scale.shape)
    for at, x0, x1 in ((0, a0, a1), (half, b0, b1)):
        added = x0[:half, :].astype(F32) + x1[:half, :].astype(F32)
        sums[at : at + half, :] = added
        result[at : at + half, :] = u[at : at + half, :].astype(F32) + factor[at : at + half] * added


def gate_back_kernel(
    width_total, heads, width, g, sums, scale, weights, ssd, gate, logs, conv_pre, params,
    grad_ssd, grad_gate, mixed, grad_gain, local_term,
):
    channels = heads * width
    state_size = (conv_pre.shape[1] - channels) // 2
    grad_q = g[...].astype(BF16)
    grad_mixed = dot(grad_q, weights[:, channels:], (1, 0))
    inner = jnp.sum(grad_q.astype(F32) * sums[...], axis=1, keepdims=True)
    factor = scale[:, 0:1]
    raw = gate[...]
    sig = sigmoid(raw)
    silu = raw * sig
    value = ssd[...]
    gated = value * silu
    scaled_gated = gated * factor
    gain = params[GATE : GATE + 1, :channels]
    mixed[...] = (scaled_gated * gain).astype(BF16)
    grad_gain[...] = jnp.broadcast_to(
        jnp.sum(grad_mixed * scaled_gated, axis=0, keepdims=True), grad_gain.shape
    )
    grad_gated = factor * (grad_mixed * gain) - scaled_gated * (factor * factor * inner / width_total)
    grad_out = grad_gated * silu
    grad_ssd[...] = grad_out
    grad_gate[...] = (grad_gated * value * (sig * (1.0 + raw * (1.0 - sig)))).astype(BF16)
    log_decay = logs[...]
    pre = conv_pre[:, channels + state_size :]
    c_rows = pre * sigmoid(pre)
    local_term[:channels, :] = mm_tn(
        grad_out * expand(jnp.exp(log_decay), heads, width), c_rows
    ).astype(BF16)
    local_term[channels:, :] = log_rows(log_decay[log_decay.shape[0] - 1 :, :]).astype(BF16)


def store_halves(scalars, low, high, kept, sent):
    low, high = low.astype(BF16), high.astype(BF16)

    @pl.when(scalars[1] == 0)
    def _():
        kept[...] = low
        sent[...] = high

    @pl.when(scalars[1] != 0)
    def _():
        kept[...] = high
        sent[...] = low


def within_back_kernel(
    heads, width, scalars, g, mixed, normed, grad_gate, grad_ssd, conv_pre, dt_raw, logs, table,
    early_kept, early_sent, grad_scaled, grad_bc, scaled, flipped, grad_products,
):
    channels = heads * width
    state_size = (conv_pre.shape[1] - channels) // 2
    store_halves(
        scalars, mm_tn(normed[HALO:, :], grad_gate[...]), mm_tn(g[...], mixed[...]), early_kept, early_sent
    )
    pre = conv_pre[...]
    out = pre * sigmoid(pre)
    b_rows = out[:, channels : channels + state_size].astype(BF16)
    c_rows = out[:, channels + state_size :].astype(BF16)
    step = softplus(dt_raw[...] + table[0:1, :])
    scaled[...] = (out[:, :channels] * expand(step, heads, width)).astype(BF16)
    products = mm_nt(b_rows, c_rows)
    log_decay = logs[...]
    flipped[...] = jnp.transpose(log_decay)
    row = lax.broadcasted_iota(jnp.int32, products.shape, 0)
    later = row <= lax.broadcasted_iota(jnp.int32, products.shape, 1)
    low = low_half(width)
    grad_products[...] = jnp.zeros_like(products)

    @pl.loop(0, heads // 2)
    def _(pair):
        lanes = pair_lanes(pair, width)
        grad_tile, tile = grad_ssd[:, lanes], scaled[:, lanes]
        parts = []
        for i in range(2):
            h = 2 * pair + i
            spread = flipped[pl.ds(h, 1), :] - head_column(log_decay, h)
            decays = jnp.exp(jnp.where(later, spread, -1e30))
            own = jnp.where(low if i == 0 else jnp.logical_not(low), grad_tile, 0.0)
            grad_products[...] += mm_nt(tile, own) * decays
            parts.append(mm(decays * products, grad_tile))
        grad_scaled[:, lanes] = jnp.where(low, parts[0], parts[1])

    grad_bc[:, :state_size] = mm(grad_products[...], c_rows)
    grad_bc[:, state_size:] = mm_tn(grad_products[...], b_rows)


def project_back_kernel(
    heads, width, kernel, count, scalars, grad_ssd, grad_scaled, grad_bc, ssd, conv_pre, conv_in, dt_raw, logs, table,
    params, incoming, normed, grad_gate, weights, gate_weights, grad_gain, *refs
):
    terms = refs[: count - 1]
    part_a, part_b, part_h, late_kept, late_sent, small, padded, wide = refs[count - 1 :]
    channels = heads * width
    length = grad_ssd.shape[0]
    mixed_width = conv_pre.shape[1]
    state_size = (mixed_width - channels) // 2
    end_grad = combine([ref[...] for ref in terms], heads, width)
    pre = conv_pre[...]
    sig = sigmoid(pre)
    out = pre * sig
    slope = sig * (1.0 + pre * (1.0 - sig))
    x_in = out[:, :channels]
    b_rows = out[:, channels : channels + state_size]
    shifted = dt_raw[...] + table[0:1, :]
    step = softplus(shifted)
    rate = -jnp.exp(table[1:2, :])
    log_decay = logs[...]
    last = log_decay[length - 1 :, :]
    step_x = expand(step, heads, width)
    skip_x = expand(table[2:3, :], heads, width)
    to_end = expand(jnp.exp(last - log_decay), heads, width)
    scaled = x_in * step_x
    grad_out = grad_ssd[...]
    pulled = mm_nt(b_rows, end_grad) * to_end
    grad_xs = grad_scaled[...] + pulled
    grad_b = grad_bc[:, :state_size] + mm(scaled * to_end, end_grad)
    grad_c = grad_bc[:, state_size:] + mm(grad_out * expand(jnp.exp(log_decay), heads, width), incoming[...])
    grad_log = head_sums(grad_out * (ssd[...] - skip_x * x_in) - scaled * grad_xs, heads, width)
    contrib = jnp.sum(scaled * pulled, axis=0, keepdims=True)
    crossed = end_grad * incoming[...]
    lane = lax.broadcasted_iota(jnp.int32, (1, LANES), 1)
    last_add = head_sums(jnp.broadcast_to(contrib, (8, channels)), heads, width)[0:1, :]
    for h in range(heads):
        amount = jnp.sum(
            jnp.sum(crossed[h * width : (h + 1) * width], axis=0, keepdims=True), axis=1, keepdims=True
        )
        last_add = last_add + jnp.where(lane == h, amount, 0.0) * jnp.exp(last)
    row = lax.broadcasted_iota(jnp.int32, (length, length), 0)
    column = lax.broadcasted_iota(jnp.int32, (length, length), 1)
    grad_steps = ordered_sums(row <= column, grad_log) + last_add
    grad_step = grad_steps * rate + head_sums(grad_xs * x_in, heads, width)
    grad_rate = jnp.sum(grad_steps * step, axis=0, keepdims=True)
    skip_terms = jnp.sum(grad_out * x_in, axis=0, keepdims=True)
    grad_skip = head_sums(jnp.broadcast_to(skip_terms, (8, channels)), heads, width)[0:1, :]
    grad_dt = grad_step * small_sigmoid(shifted)
    grad_x = grad_xs * step_x + skip_x * grad_out
    padded[:HALO, :] = jnp.zeros((HALO, mixed_width), F32)
    padded[HALO + length :, :] = jnp.zeros((HALO, mixed_width), F32)
    padded[HALO : HALO + length, :channels] = grad_x * slope[:, :channels]
    padded[HALO : HALO + length, channels : channels + state_size] = (
        grad_b * slope[:, channels : channels + state_size]
    )
    padded[HALO : HALO + length, channels + state_size :] = grad_c * slope[:, channels + state_size :]
    grad_pre = padded[HALO : HALO + length, :]
    small[...] = jnp.zeros(small.shape, F32)
    grad_v = jnp.zeros((HALO + length, mixed_width), F32)
    for k in range(kernel):
        small[k : k + 1, :mixed_width] = jnp.sum(
            grad_pre * conv_in[pl.ds(HALO - kernel + 1 + k, length), :], axis=0, keepdims=True
        )
        grad_v = grad_v + params[k : k + 1, :mixed_width] * padded[pl.ds(kernel - 1 - k, HALO + length), :]
    small[kernel : kernel + 1, :mixed_width] = jnp.sum(grad_pre, axis=0, keepdims=True)
    small[GATE : GATE + 1, :channels] = grad_gain[0:1, :]
    small[TABLE : TABLE + 1, :LANES] = jnp.sum(grad_dt, axis=0, keepdims=True)
    small[TABLE + 1 : TABLE + 2, :LANES] = grad_rate * rate
    small[TABLE + 2 : TABLE + 3, :LANES] = grad_skip
    wide[:, :mixed_width] = grad_v.astype(BF16)
    wide[:HALO, mixed_width:] = jnp.zeros((HALO, LANES), BF16)
    wide[HALO:, mixed_width:] = grad_dt.astype(BF16)
    grad_late = mm_tn(normed[...], wide[...])
    store_halves(scalars, grad_late[:, :channels], grad_late[:, channels:], late_kept, late_sent)
    rest = dot(wide[...], weights[...], (1, 1))
    part = rest[HALO:, :] + dot(grad_gate[...], gate_weights[:, :channels], (1, 1))
    half = length // 2
    both = mixed_width - channels
    part_a[:half, :] = part[:half].astype(BF16)
    part_a[half:, :] = jnp.zeros((HALO, part_a.shape[1]), BF16)
    part_a[half:, : 3 * both] = split_lanes(small[:, channels:mixed_width])
    part_b[...] = part[half:].astype(BF16)
    part_h[...] = rest[:HALO, :].astype(BF16)


def norm_back_kernel(kernel, channels, both, half, g, u, params, a0, a1, b0, b1, *refs):
    *smalls, grad_u, all_small = refs
    gain = params[GAIN : GAIN + 1, :]
    for i, ref in enumerate(smalls):
        all_small[i * ROWS : (i + 1) * ROWS, :] = ref[...]
    all_small[GAIN : GAIN + 1, :] = jnp.zeros_like(gain)
    chunk = 2 * HALO
    for at, x0, x1 in ((0, a0, a1), (half, b0, b1)):

        @pl.loop(0, half // chunk)
        def _(i):
            here = pl.ds(pl.multiple_of(i * chunk, chunk), chunk)
            there = pl.ds(pl.multiple_of(at + i * chunk, chunk), chunk)
            normed = x0[here, :].astype(F32) + x1[here, :].astype(F32)
            rows = u[there, :].astype(F32)
            inv = lax.rsqrt(jnp.mean(rows * rows, axis=1, keepdims=True) + EPSILON)
            all_small[GAIN : GAIN + 1, :] += jnp.sum(normed * rows * inv, axis=0, keepdims=True)
            scaled = normed * gain
            mean = jnp.mean(scaled * rows, axis=1, keepdims=True)
            grad_u[there, :] = (
                g[there, :].astype(F32) + inv * scaled - rows * (inv * inv * inv * mean)
            )

    shared = join_lanes(a0[half:, :], both) + join_lanes(a1[half:, :], both)
    all_small[: kernel + 1, channels : channels + both] = shared[: kernel + 1]


def place_kernel(scalars, value_0, value_1, got, out, sems):
    core = scalars[1]

    def copy(source, slot):
        return pltpu.make_async_copy(source, out.at[0, slot], sems.at[slot])

    @pl.when(core == 0)
    def _():
        copy(value_0, 0).start()
        copy(got, 1).start()

    @pl.when(core != 0)
    def _():
        copy(got, 0).start()
        copy(value_1, 1).start()

    copy(value_0, 0).wait()
    copy(value_1, 1).wait()


def finish_kernel(count, scalars, *refs):
    both_1, early_0, late_0 = refs[:count], refs[count : 2 * count], refs[2 * count : 3 * count]
    own, other = refs[3 * count :]
    columns = early_0[0].shape[1]

    rows = own.shape[0]
    chunk = rows // 4 if rows % (4 * HALO) == 0 else rows

    def write(section_0, section_1):
        @pl.loop(0, rows // chunk)
        def _(i):
            here = pl.ds(pl.multiple_of(i * chunk, HALO), chunk)

            def total(pieces):
                return sum(ref[here, :].astype(F32) for ref in pieces)

            section_0[here, :columns] = total(early_0)
            section_0[here, columns:] = total(late_0)
            section_1[here, :] = total(both_1)

    @pl.when(scalars[1] == 0)
    def _():
        write(own, other)

    @pl.when(scalars[1] != 0)
    def _():
        write(other, own)


def call(body, outs, inputs, anywhere=(), scratch=(), scalars=False, flops=0, out_space=pltpu.VMEM):
    in_specs = [
        pl.BlockSpec(memory_space=pl.ANY if i in anywhere else pltpu.VMEM) for i in range(len(inputs))
    ]
    if scalars:
        in_specs[0] = pl.BlockSpec(memory_space=pltpu.SMEM)
    shapes = [jax.ShapeDtypeStruct(shape, dtype) for shape, dtype in outs]
    moved = sum(x.size * x.dtype.itemsize for x in list(inputs) + shapes)
    return pl.pallas_call(
        body,
        out_shape=shapes,
        in_specs=in_specs,
        out_specs=[pl.BlockSpec(memory_space=out_space)] * len(shapes),
        scratch_shapes=list(scratch),
        cost_estimate=pl.CostEstimate(flops=flops, bytes_accessed=moved, transcendentals=0),
        compiler_params=pltpu.CompilerParams(vmem_limit_bytes=VMEM_LIMIT),
    )(*inputs)


def rotate(x, k):
    size = lax.axis_size(CTX)
    return lax.ppermute(x, CTX, [(i, (i + k) % size) for i in range(size)])


def shifted(x, k):
    size = lax.axis_size(CTX)
    return lax.ppermute(x, CTX, [(i, i + k) for i in range(size) if 0 <= i + k < size])


def swap_cores(x):
    return lax.ppermute(x, SECTION, [(0, 1), (1, 0)])


def partner(x, bits):
    size = lax.axis_size(TENSOR)
    return lax.ppermute(x, TENSOR, [(i, i ^ bits) for i in range(size)])


def tensor_bits():
    size = lax.axis_size(TENSOR)
    return [1 << i for i in range(size.bit_length() - 1)]


def exchange(a, b, add):
    bits = tensor_bits()
    for i, bit in enumerate(bits):
        other_a, other_b = partner(a, bit), partner(b, bits[-1 - i])
        if i == len(bits) - 1:
            return a, other_a, b, other_b
        a, b = add(a, other_a, b, other_b, i)


def tensor_sum(x):
    for bit in tensor_bits():
        x = x + partner(x, bit)
    return x


def ctx_sum(x):
    size = lax.axis_size(CTX)
    terms = [x] + [lax.ppermute(x, CTX, [(i, i ^ k) for i in range(size)]) for k in range(1, size)]
    while len(terms) > 1:
        terms = [terms[i] + terms[i + 1] for i in range(0, len(terms), 2)]
    return terms[0]


def crossed_pairs(k):
    length, size = lax.axis_size(CTX), lax.axis_size(TENSOR)
    bit = tensor_bits()[-1]
    return [
        (i * size + j, (i + k) * size + (j ^ bit))
        for i in range(length) if 0 <= i + k < length for j in range(size)
    ]


def over_cores(kept, sent):
    return kept + swap_cores(sent)


def scatter_start(totals, position):
    size = lax.axis_size(CTX)
    rows = totals[0].shape[0] // size

    def piece(k):
        start = lax.rem(position + k, size) * rows
        parts = [lax.dynamic_slice_in_dim(total, start, rows, axis=0) for total in totals]
        return parts[0] if len(parts) == 1 else jnp.concatenate(parts, axis=1)

    return [piece(0)] + [rotate(piece(k), k) for k in range(1, size)]


def local(
    block_input, out_grad, norm_gain, w_zx, w_bc, w_dt, conv_x, conv_x_bias, conv_bc, conv_bc_bias,
    head_params, gate_gain, w_out,
):
    count = lax.axis_size(CTX)
    core, position = lax.axis_index(SECTION), lax.axis_index(CTX)
    scalars = jnp.stack([position, core]).astype(jnp.int32)
    length, model = block_input.shape[1:]
    shard = w_zx.shape[1]
    heads, width = conv_x.shape[2], conv_x.shape[3] * count
    channels = heads * width
    kernel = conv_x.shape[1]
    both = w_bc.shape[2]
    mixed_width = channels + both
    width_total = channels * lax.axis_size(TENSOR)
    half = length // 2

    own_u = lax.dynamic_index_in_dim(block_input, core, 0, keepdims=False)
    own_g = lax.dynamic_index_in_dim(out_grad, core, 0, keepdims=False)
    halo_0 = shifted(own_u[length - HALO :], 1)

    first_core = core == 0
    first_weights = jnp.concatenate(
        [w_zx[0, :, 1], w_bc[0], jnp.pad(w_dt[0], ((0, 0), (0, LANES - heads)))], axis=1
    )
    second_weights = jnp.concatenate([w_zx[0, :, 0], jnp.transpose(w_out[0])], axis=1)

    def halves(x):
        low, high = x[:, : x.shape[1] // 2], x[:, x.shape[1] // 2 :]
        kept, sent = jnp.where(first_core, low, high), jnp.where(first_core, high, low)
        got = swap_cores(sent)
        return [jnp.where(first_core, kept, got), jnp.where(first_core, got, kept)], got

    first_halves, got_half = halves(first_weights)
    second_halves, _ = halves(second_weights)

    def spread_out(x):
        pieces = [x] + [rotate(x, k) for k in range(1, count)]
        return pieces + [swap_cores(piece) for piece in pieces]

    first_pieces = [spread_out(half) for half in first_halves]
    second_pieces = [spread_out(half) for half in second_halves]

    (conv_x, conv_x_bias, conv_bc, conv_bc_bias, norm_gain, gate_gain, head_params), got_half = (
        lax.optimization_barrier(
            ((conv_x, conv_x_bias, conv_bc, conv_bc_bias, norm_gain, gate_gain, head_params), got_half)
        )
    )

    def at_home(x):
        full = jnp.zeros(x.shape[:-1] + (x.shape[-1] * count,), x.dtype)
        return lax.dynamic_update_slice_in_dim(full, x, position * x.shape[-1], axis=x.ndim - 1)

    by_head = at_home(jnp.concatenate([conv_x[0], conv_x_bias, gate_gain], axis=0)).reshape(
        kernel + 2, channels
    )
    by_state = at_home(jnp.concatenate([conv_bc[0], conv_bc_bias], axis=0))
    by_model = at_home(norm_gain)

    def filled(rows, lanes):
        return jnp.zeros((rows, lanes), BF16)

    conv_rows = jnp.concatenate(
        [by_head[: kernel + 1], by_state, filled(kernel + 1, model - mixed_width)], axis=1
    )
    gate_row = jnp.concatenate([by_head[kernel + 1 :], filled(1, model - channels)], axis=1)
    own_block = jnp.concatenate([conv_rows, by_model, gate_row, filled(ROWS - kernel - 3, model)], axis=0)
    own_table = jnp.pad(head_params[0], ((0, 8 - head_params.shape[1]), (0, LANES - heads)))
    other_block, other_table = swap_cores(own_block), swap_cores(own_table)
    pair = jnp.concatenate(
        [jnp.where(first_core, own_block, other_block), jnp.where(first_core, other_block, own_block)],
        axis=0,
    )
    tables = [
        jnp.where(first_core, own_table, other_table), jnp.where(first_core, other_table, own_table)
    ]
    blocks = [pair] + [rotate(pair, k) for k in range(1, count)]

    dma = pltpu.SemaphoreType.DMA((2, count))
    ext = length + HALO
    pair_scratch = [pltpu.VMEM((length, channels), BF16), pltpu.VMEM((LANES, length), F32)]
    state_shape = ((channels + HALO, LANES), BF16)
    rows_f32 = ((length, channels), F32)

    def forward(section, u, halo, with_halo):
        table = tables[section]
        weights, params, normed, conv_in, conv_pre, dt_raw, logs, state = call(
            functools.partial(project_kernel, section, heads, width, kernel, count),
            [
                ((model, first_weights.shape[1]), BF16), ((ROWS, model), F32), ((ext, model), BF16),
                ((ext, mixed_width), F32), ((length, mixed_width), F32), ((length, LANES), F32),
                ((length, LANES), F32), state_shape,
            ],
            [scalars, u, halo, table] + blocks + first_pieces[section],
            scratch=[dma], scalars=True,
            flops=2 * ext * model * first_weights.shape[1],
        )
        states = [shifted(state, k) for k in range(1, count)]
        within, gate_weights, gate = call(
            functools.partial(within_kernel, heads, width, count),
            [rows_f32, ((model, second_weights.shape[1]), BF16), rows_f32],
            [scalars, conv_pre, dt_raw, logs, table, normed] + second_pieces[section],
            scratch=[dma, *pair_scratch], scalars=True,
            flops=2 * length * length * (LANES * heads + LANES),
        )
        incoming, ssd, part_a, part_b, part_h = call(
            functools.partial(out_kernel, heads, width),
            [
                ((channels, LANES), F32), rows_f32,
                ((half + HALO, model), BF16), ((half, model), BF16), ((2 * HALO, model), BF16),
            ],
            [within, conv_pre, gate, logs, table, params, gate_weights] + states,
            flops=2 * length * model * channels,
        )
        tails = []
        if with_halo:
            tails = [
                shifted(part_h, 1), lax.ppermute(part_h, (CTX, TENSOR), crossed_pairs(1))
            ]

        def add(a0, a1, b0, b1, step):
            return call(
                functools.partial(first_sum_kernel, length, half),
                [(a0.shape, BF16), ((half + HALO * len(tails), model), BF16)],
                [a0, a1, b0, b1] + tails,
            )

        extra = [halo] if with_halo else []
        result, sums, scale, *next_halo = call(
            functools.partial(add_kernel, width_total, half),
            [((length, model), F32), ((length, model), F32), ((length, LANES), F32)]
            + [((HALO, model), F32)] * len(extra),
            [u, *exchange(part_a, part_b, add), *extra],
        )
        kept = (
            u, weights, gate_weights, params, normed, gate, conv_in, conv_pre, dt_raw, logs, incoming, ssd,
            sums, scale,
        )
        return result, kept, next_halo

    def backward(section, g, kept, smalls):
        table = tables[section]
        (
            u, weights, gate_weights, params, normed, gate, conv_in, conv_pre, dt_raw, logs, incoming, ssd,
            sums, scale,
        ) = kept
        grad_ssd, grad_gate, mixed, grad_gain, local_term = call(
            functools.partial(gate_back_kernel, width_total, heads, width),
            [rows_f32, ((length, channels), BF16), ((length, channels), BF16), ((8, channels), F32), state_shape],
            [g, sums, scale, gate_weights, ssd, gate, logs, conv_pre, params],
            flops=2 * length * model * channels,
        )
        terms = [shifted(local_term, -k) for k in range(1, count)]
        early_kept, early_sent, grad_scaled, grad_bc = call(
            functools.partial(within_back_kernel, heads, width),
            [((model, channels), BF16), ((model, channels), BF16), rows_f32, ((length, both), F32)],
            [scalars, g, mixed, normed, grad_gate, grad_ssd, conv_pre, dt_raw, logs, table],
            scratch=[*pair_scratch, pltpu.VMEM((length, length), F32)],
            scalars=True, flops=4 * length * model * channels,
        )
        early = over_cores(early_kept, early_sent)
        if section == 0:
            early_pieces = scatter_start([early], position)
        part_a, part_b, part_h, late_kept, late_sent, small_grads = call(
            functools.partial(project_back_kernel, heads, width, kernel, count),
            [
                ((half + HALO, model), BF16), ((half, model), BF16), ((HALO, model), BF16),
                ((model, channels), BF16), ((model, channels), BF16), ((ROWS, model), F32),
            ],
            [
                scalars, grad_ssd, grad_scaled, grad_bc, ssd, conv_pre, conv_in, dt_raw, logs, table,
                params, incoming, normed, grad_gate, weights, gate_weights, grad_gain, *terms,
            ],
            scratch=[
                pltpu.VMEM((length + 2 * HALO, mixed_width), F32),
                pltpu.VMEM((ext, mixed_width + LANES), BF16),
            ],
            scalars=True, flops=6 * length * model * 2 * channels,
        )
        tails = [shifted(part_h, -1), lax.ppermute(part_h, (CTX, TENSOR), crossed_pairs(-1))]

        def add(a0, a1, b0, b1, step):
            return call(
                functools.partial(first_sum_back_kernel, both, half), [(a0.shape, BF16), (b0.shape, BF16)],
                [a0, a1, b0, b1] + tails,
            )

        late = over_cores(late_kept, late_sent)
        if section == 0:
            pieces = (early_pieces, scatter_start([late], position))
        else:
            pieces = scatter_start([early, late], position)
        smalls = [small_grads] + smalls
        grad_u, all_small = call(
            functools.partial(norm_back_kernel, kernel, channels, both, half),
            [((length, model), F32), ((ROWS * len(smalls), model), F32)],
            [g, u, params, *exchange(part_a, part_b, add), *smalls],
        )
        return grad_u, pieces, all_small

    out_0, kept_0, next_halo = forward(0, own_u, halo_0, True)
    out_1, kept_1, _ = forward(1, out_0, next_halo[0], False)
    grad_1, pieces_1, small_1 = backward(1, own_g, kept_1, [])
    grad_0, pieces_0, small_0 = backward(0, grad_1, kept_0, [small_1])

    def placed(value_0, value_1):
        got = swap_cores(jnp.where(first_core, value_1, value_0))
        return call(
            place_kernel, [((1, 2, length, model), F32)], [scalars, value_0, value_1, got],
            scratch=[pltpu.SemaphoreType.DMA((2,))], scalars=True, out_space=pl.ANY,
        )[0]

    block_output = placed(out_0, out_1)
    input_grad = placed(grad_0, grad_1)
    small_0 = small_0 + swap_cores(small_0)
    total = ctx_sum(small_0)
    pieces_0, total = lax.optimization_barrier((pieces_0, total))
    small = jnp.where(first_core, total[:ROWS], total[ROWS:])
    wide_shape = ((shard, 2 * channels), F32)
    mine, other = call(
        functools.partial(finish_kernel, count), [wide_shape, wide_shape],
        [scalars, *pieces_1, *pieces_0[0], *pieces_0[1]], scalars=True,
    )
    got = swap_cores(other)
    own_early, own_late = mine[:, :channels], mine[:, channels:]
    got_early, got_late = got[:, :channels], got[:, channels:]
    z_grad = jnp.where(first_core, own_early, got_early)
    out_w_grad = jnp.where(first_core, got_early, own_early)
    x_grad = jnp.where(first_core, own_late, got_late)
    rest_grad = jnp.where(first_core, got_late, own_late)
    bc_grad = tensor_sum(rest_grad[:, :both])
    dt_grad = rest_grad[:, both : both + heads]

    def own(value, axis):
        size = value.shape[axis] // count
        return lax.dynamic_slice_in_dim(value, position * size, size, axis=axis)[None]

    norm_grad = own(small[GAIN], 0)
    x_grads = own(small[:ROWS // 2, :channels].reshape(ROWS // 2, heads, width), 2)
    bc_grads = own(small[: ROWS // 2, channels:mixed_width], 1)
    head_grad = small[TABLE : TABLE + 3, :heads][None]
    gain_grad = x_grads[:, GATE]
    zx_grad = jnp.stack([z_grad, x_grad], axis=1)[None]
    return (
        block_output,
        input_grad,
        norm_grad,
        zx_grad,
        bc_grad[None],
        dt_grad[None],
        x_grads[:, :kernel],
        x_grads[:, kernel],
        bc_grads[:, :kernel],
        bc_grads[:, kernel],
        head_grad,
        gain_grad,
        jnp.transpose(out_w_grad)[None],
    )


def solution(mesh):
    in_specs = (
        P(None, CTX, None),
        P(None, CTX, None),
        P(SECTION, CTX),
        P(SECTION, CTX, None, TENSOR),
        P(SECTION, CTX, None),
        P(SECTION, CTX, TENSOR),
        P(SECTION, None, TENSOR, CTX),
        P(SECTION, TENSOR, CTX),
        P(SECTION, None, CTX),
        P(SECTION, CTX),
        P(SECTION, None, TENSOR),
        P(SECTION, TENSOR, CTX),
        P(SECTION, TENSOR, CTX),
    )
    out_specs = (
        P(SECTION, None, CTX, None),
        P(SECTION, None, CTX, None),
        *in_specs[2:],
    )

    return jax.shard_map(local, mesh=mesh, in_specs=in_specs, out_specs=out_specs, check_vma=False)
```
